32 devices in a mesh: ctx: 8 (over y, x, core), pipe: 4 (over z).
Axes of the slice: x: 2, y: 2, z: 4, core: 2. Of those that a mesh axis runs over, the one named last changes fastest.
Arguments:
- tokens: bfloat16 [1, 1024, 2048], P(None, 'ctx'), may hold values from -6 to 6
- w_qkv: bfloat16 [4, 16, 128, 384], P('pipe'), may hold values from -0.5 to 0.5
- norm_gain: float32 [4, 2048], P('pipe'), may hold values from 0.5 to 1.5
- out_gain: float32 [4, 2048], P('pipe'), may hold values from 0.5 to 1.5
Outputs:
- hidden: bfloat16 [4, 1, 1024, 2048], P('pipe', None, 'ctx')
The draws below stay inside these ranges and needn't reach their ends.
All inputs are finite; a program needn't handle non-finite values.
Results may differ from the reference program's by a relative error of at most 0.03.
Values may be sent and summed in bfloat16 or wider, within the bound.
A program may use at most 128 MiB of HBM per device.

```python
import jax
import jax.numpy as jnp
from jax import lax

HEADS = 16
HEAD_DIM = 128
D = 2048
TOK_DEV = 128
MB = 1
TOKENS = 1024
LAYERS = 4


def levels(rng, dims, pieces, least, largest):
    def one(dim, parts):
        draws = jax.random.uniform(jax.random.fold_in(jax.random.fold_in(rng, 6), dim), (parts,), jnp.float32, least / len(pieces), largest / len(pieces))
        return jnp.repeat(jnp.exp(draws), dims[dim] // parts).reshape((-1,) + (1,) * (len(dims) - dim - 1))

    gain = one(*pieces[0])
    for cut in pieces[1:]:
        gain = gain * one(*cut)
    return gain


def centred(own_key, shape, spread, most, split=(), kind=jnp.bfloat16):
    entries = spread * jax.random.normal(own_key, shape, jnp.float32)
    if split:
        entries = entries * levels(own_key, shape, split, -0.22, 0.18)
    return jnp.clip(entries, -most, most).astype(kind)


def setup_inputs(seed: int = 0) -> dict:
    streams_of = jax.random.split(jax.random.key(seed), 5)
    return {
        "tokens": centred(streams_of[0], (MB, TOKENS, D), 1.0, 6.0, ((1, 8),)),
        "w_qkv": centred(streams_of[1], (LAYERS, HEADS, HEAD_DIM, 3 * HEAD_DIM), HEAD_DIM ** -0.5, 0.5, ((0, 4),)),
        "norm_gain": jnp.clip(0.5 + 1.0 * jax.random.uniform(streams_of[2], (LAYERS, D), jnp.float32) ** levels(streams_of[2], (LAYERS, D), ((0, 4),), -0.2, 0.2), 0.5, 1.5),
        "out_gain": jnp.clip(0.5 + 1.0 * jax.random.uniform(streams_of[3], (LAYERS, D), jnp.float32) ** levels(streams_of[3], (LAYERS, D), ((0, 4),), -0.2, 0.2), 0.5, 1.5),
    }


epsilon = 1e-06

def rounded(value):
    return lax.optimization_barrier(value.astype(jnp.bfloat16)).astype(jnp.float32)

def one_layer(stream, gain_in, weights, gain_out):
    length = stream.shape[0]
    head_count = weights.shape[0]
    head_dim = weights.shape[1]
    widened = stream.astype(jnp.float32)
    normed = rounded(widened * lax.rsqrt(lax.optimization_barrier(jnp.mean(widened * widened, -1, keepdims=True)) + epsilon) * gain_in)
    projected = jnp.einsum('thd,hde->hte', normed.reshape(length, head_count, head_dim), weights.astype(jnp.float32))
    queries = rounded(projected[..., :head_dim] * head_dim ** (-0.5))
    keys_all = rounded(projected[..., head_dim:2 * head_dim])
    values_all = rounded(projected[..., 2 * head_dim:])
    blocks = length // TOK_DEV
    query_blocks = queries.reshape(head_count, blocks, TOK_DEV, head_dim)
    key_blocks = keys_all.reshape(head_count, blocks, TOK_DEV, head_dim)
    value_blocks = values_all.reshape(head_count, blocks, TOK_DEV, head_dim)
    kv_state = jnp.einsum('hbte,hbtf->hbef', key_blocks, value_blocks)
    running = jnp.cumsum(kv_state, axis=1)
    prefix = jnp.concatenate([jnp.zeros((head_count, 1, head_dim, head_dim), jnp.float32), running[:, :-1]], axis=1)
    prefix = rounded(prefix)
    scores = jnp.einsum('hbte,hbse->hbts', query_blocks, key_blocks)
    positions = jnp.arange(TOK_DEV, dtype=jnp.int32)
    causal = positions[:, None] >= positions[None, :]
    masked = rounded(jnp.where(causal, scores, 0.0))
    mixed_heads = jnp.einsum('hbts,hbsf->hbtf', masked, value_blocks) + jnp.einsum('hbte,hbef->hbtf', query_blocks, prefix)
    mixed_heads = mixed_heads * lax.rsqrt(lax.optimization_barrier(jnp.mean(mixed_heads * mixed_heads, -1, keepdims=True)) + epsilon)
    branch = jnp.transpose(mixed_heads.reshape(head_count, length, head_dim), (1, 0, 2)).reshape(length, head_count * head_dim)
    return (widened + branch * gain_out).astype(jnp.bfloat16)

def reference(tokens, w_qkv, norm_gain, out_gain):
    layer_outputs = []
    for layer_index in range(LAYERS):
        sequence_outputs = []
        for sequence_index in range(MB):
            stream = tokens[sequence_index] if layer_index == 0 else layer_outputs[-1][sequence_index]
            sequence_outputs.append(one_layer(stream, norm_gain[layer_index], w_qkv[layer_index], out_gain[layer_index]))
        layer_outputs.append(jnp.stack(sequence_outputs, 0))
    return jnp.stack(layer_outputs, 0)
```

```python
import functools

import jax
import jax.numpy as jnp
from jax import lax
from jax.experimental import pallas as pl
from jax.experimental.pallas import tpu as pltpu
from jax.sharding import PartitionSpec as P

epsilon = 1e-06


def shifted(block, axis, distance):
    devices = range(lax.axis_size(axis))
    route = [(i - distance, i) for i in devices if i - distance in devices]
    return lax.ppermute(block, axis, route)


def run_layer(stream, gain_in, weights, gain_out):
    row_count = stream.shape[0]
    head_count = weights.shape[0]
    head_dim = weights.shape[1]
    widened = stream.astype(jnp.float32)
    normed = (
        widened * lax.rsqrt(jnp.mean(widened * widened, -1, keepdims=True) + epsilon) * gain_in
    ).astype(jnp.bfloat16)
    projected = jnp.einsum(
        "thd,hde->hte",
        normed.reshape(row_count, head_count, head_dim),
        weights,
        preferred_element_type=jnp.float32,
    )
    queries = (projected[..., :head_dim] * head_dim ** (-0.5)).astype(jnp.bfloat16)
    keys_local = projected[..., head_dim : 2 * head_dim].astype(jnp.bfloat16)
    values_local = projected[..., 2 * head_dim :].astype(jnp.bfloat16)
    kv_state = jnp.einsum(
        "hte,htf->hef", keys_local, values_local, preferred_element_type=jnp.float32
    )
    flat_state = kv_state.reshape(1, head_count * head_dim, head_dim)
    spread = lax.all_to_all(
        flat_state.astype(jnp.bfloat16), "ctx", split_axis=1, concat_axis=0, tiled=True
    ).astype(flat_state.dtype)
    running = jnp.cumsum(spread, axis=0)
    lower = jnp.concatenate([jnp.zeros_like(spread[:1]), running[:-1]], axis=0)
    returned = lax.all_to_all(
        lower.astype(jnp.bfloat16), "ctx", split_axis=0, concat_axis=1, tiled=True
    ).astype(lower.dtype)
    prefix = returned.reshape(kv_state.shape)
    scores = jnp.einsum("hte,hse->hts", queries, keys_local, preferred_element_type=jnp.float32)
    positions = jnp.arange(row_count, dtype=jnp.int32)
    causal = positions[:, None] >= positions[None, :]
    masked = jnp.where(causal, scores, 0.0).astype(jnp.bfloat16)
    mixed_heads = jnp.einsum(
        "hts,hsf->htf", masked, values_local, preferred_element_type=jnp.float32
    )
    mixed_heads = mixed_heads + jnp.einsum(
        "hte,hef->htf", queries, prefix.astype(jnp.bfloat16), preferred_element_type=jnp.float32
    )
    mixed_heads = mixed_heads * lax.rsqrt(
        jnp.mean(mixed_heads * mixed_heads, -1, keepdims=True) + epsilon
    )
    branch = jnp.transpose(mixed_heads, (1, 0, 2)).reshape(row_count, head_count * head_dim)
    return (widened + branch * gain_out).astype(jnp.bfloat16)


def shards(tokens, w_qkv, norm_gain, out_gain):
    section_count = lax.axis_size("pipe")
    section_index = lax.axis_index("pipe")
    micro_count = tokens.shape[0]
    hidden_buffer = jnp.zeros(tokens.shape, jnp.bfloat16)
    carried = jnp.zeros(tokens.shape[1:], jnp.bfloat16)
    total_steps = micro_count + section_count - 1
    for tick_index in range(total_steps):
        fresh = tokens[min(tick_index, micro_count - 1)]
        layer_input = jnp.where(section_index == 0, fresh, carried)
        result = run_layer(layer_input, norm_gain[0], w_qkv[0], out_gain[0])
        micro_index = tick_index - section_index
        usable = (micro_index >= 0) & (micro_index < micro_count)
        slot_index = jnp.clip(micro_index, 0, micro_count - 1)
        previous = lax.dynamic_index_in_dim(hidden_buffer, slot_index, 0, keepdims=False)
        hidden_buffer = lax.dynamic_update_index_in_dim(
            hidden_buffer, jnp.where(usable, result, previous), slot_index, 0
        )
        if tick_index + 1 < total_steps:
            carried = shifted(result, "pipe", 1)
    return hidden_buffer[None]


MESH = pl.DeviceIdType.MESH
FAR_FIRST = (6, 7, 2, 4, 3, 5, 1)


def partner(index, flips):
    total = 0
    for bit in (1, 2, 4):
        own = lax.rem(index // bit, 2)
        total = total + (lax.rem(own + 1, 2) if flips & bit else own) * bit
    return total


def lanes_to_rows(row):
    return jnp.broadcast_to(row, (128, row.shape[1])).T


def row_sums(values):
    upper = values.astype(jnp.bfloat16)
    lower = (values - upper.astype(jnp.float32)).astype(jnp.bfloat16)
    ones = jnp.ones((256, 128), jnp.bfloat16)
    return jnp.dot(
        jnp.concatenate([upper, lower], 1), ones, preferred_element_type=jnp.float32
    )


def relay_kernel(
    sizes,
    tok_ref,
    w_ref,
    gin_ref,
    gout_ref,
    out_ref,
    own,
    stream,
    weights,
    gains_in,
    gains_out,
    qkv,
    prefix,
    squares,
    local_sem,
    tok_send,
    tok_recv,
    sq_send,
    sq_recv,
    w_send,
    w_recv,
    out_send,
    out_recv,
):
    ctx_size, sections, heads, dim, tokens = sizes
    width = heads * dim
    features = ctx_size * width
    c = lax.axis_index("ctx")
    z = lax.axis_index("pipe")

    def cols(device):
        return pl.ds(pl.multiple_of(device * width, width), width)

    def rows(device):
        return pl.ds(pl.multiple_of(device * tokens, tokens), tokens)

    my_heads = pl.ds(c * heads, heads)

    local = [
        pltpu.make_async_copy(tok_ref.at[0], own, local_sem.at[0]),
        pltpu.make_async_copy(tok_ref.at[0, :, cols(c)], stream.at[rows(c)], local_sem.at[1]),
        pltpu.make_async_copy(w_ref.at[0, my_heads], weights.at[z], local_sem.at[2]),
        pltpu.make_async_copy(gin_ref.at[:, cols(c)], gains_in.at[z], local_sem.at[3]),
        pltpu.make_async_copy(gout_ref.at[:, cols(c)], gains_out.at[z], local_sem.at[4]),
    ]
    for copy in local:
        copy.start()

    barrier = pltpu.get_barrier_semaphore()
    for d in FAR_FIRST:
        pl.semaphore_signal(barrier, 1, device_id=(partner(c, d), z), device_id_type=MESH)
    for step in range(1, sections):
        other = lax.rem(z + step, sections)
        pl.semaphore_signal(barrier, 1, device_id=(c, other), device_id_type=MESH)
    pl.semaphore_wait(barrier, ctx_size + sections - 2)

    def tok_copy(d):
        to = partner(c, d)
        return pltpu.make_async_remote_copy(
            tok_ref.at[0, :, cols(to)], stream.at[rows(c)],
            tok_send.at[d], tok_recv.at[d], device_id=(to, z), device_id_type=MESH,
        )

    def sq_copy(layer, d):
        return pltpu.make_async_remote_copy(
            squares.at[layer, c], squares.at[layer, c],
            sq_send.at[layer, d], sq_recv.at[layer, d],
            device_id=(partner(c, d), z), device_id_type=MESH,
        )

    def w_copies(layer, to, slot, relayed):
        pieces = (
            (weights.at[layer], weights.at[layer]) if relayed else (w_ref.at[0, my_heads], weights.at[layer]),
            (gains_in.at[layer], gains_in.at[layer]) if relayed else (gin_ref.at[:, cols(c)], gains_in.at[layer]),
            (gains_out.at[layer], gains_out.at[layer]) if relayed else (gout_ref.at[:, cols(c)], gains_out.at[layer]),
        )
        return [
            pltpu.make_async_remote_copy(
                source, target, w_send.at[slot, i], w_recv.at[layer, i],
                device_id=(c, to), device_id_type=MESH,
            )
            for i, (source, target) in enumerate(pieces)
        ]

    last = sections - 1
    plan = {"start": [], "early": [], "late": [], "relay": []}
    plan["start"].append((0, 0, last, 0))
    for layer in range(1, last - 1):
        plan["early"].append((layer, layer, last, 0))
    plan["late"].append((last - 1, last - 1, last, 0))
    for layer in range(last - 1):
        for slot, to in enumerate(range(layer + 1, last)):
            if not (layer == 0 and to == last - 1 and last > 2):
                plan["late"].append((layer, layer, to, slot + 1))
    if last > 2:
        plan["relay"].append((last, 0, last - 1, 0))

    def send_weights(stage):
        for sender, layer, to, slot in plan[stage]:
            @pl.when(z == sender)
            def _():
                for copy in w_copies(layer, to, slot, stage == "relay"):
                    copy.start()

    send_weights("start")
    for d in FAR_FIRST:
        tok_copy(d).start()

    local[0].wait()
    folded = jnp.zeros((tokens, 128), jnp.float32)
    for i in range(features // 128):
        piece = own[:, i * 128 : (i + 1) * 128].astype(jnp.float32)
        folded = folded + piece * piece
    total = jnp.sum(folded.T, 0, keepdims=True)
    which = lax.broadcasted_iota(jnp.int32, (ctx_size, tokens), 0)
    squares[0, c] = jnp.where(which == c, jnp.broadcast_to(total, (ctx_size, tokens)), 0.0)
    for d in FAR_FIRST:
        sq_copy(0, d).start()
    for d in FAR_FIRST[:2]:
        tok_copy(d).wait_recv()
    send_weights("early")
    for d in FAR_FIRST[2:]:
        tok_copy(d).wait_recv()
    for copy in local[1:]:
        copy.wait()
    send_weights("late")

    at_row = lax.broadcasted_iota(jnp.int32, (tokens, tokens), 0)
    at_col = lax.broadcasted_iota(jnp.int32, (tokens, tokens), 1)
    causal = at_row >= at_col

    def out_copy(d):
        to = partner(c, d)
        return pltpu.make_async_remote_copy(
            stream.at[rows(to)], out_ref.at[0, 0, :, cols(c)],
            out_send.at[d], out_recv.at[d], device_id=(to, z), device_id_type=MESH,
        )

    def own_out():
        return pltpu.make_async_copy(
            stream.at[rows(c)], out_ref.at[0, 0, :, cols(c)], local_sem.at[0]
        )

    def one_layer(layer, carry):
        @pl.when(layer < z)
        def _():
            for copy in w_copies(layer, z, 0, True):
                copy.wait_recv()

        @pl.when(layer == 0)
        def _():
            send_weights("relay")

        for d in FAR_FIRST:
            sq_copy(layer, d).wait_recv()
        scale = lax.rsqrt(jnp.sum(squares[layer], 0) * (1.0 / features) + epsilon)
        running = [jnp.zeros((dim, dim), jnp.float32) for _ in range(heads)]
        for block in range(ctx_size):
            here = slice(block * tokens, (block + 1) * tokens)
            by_row = lanes_to_rows(scale[block : block + 1, :])
            for h in range(heads):
                mine = slice(h * dim, (h + 1) * dim)
                normed = (
                    stream[here, mine].astype(jnp.float32) * by_row * gains_in[layer, :, mine]
                ).astype(jnp.bfloat16)
                projected = jnp.dot(
                    normed, weights[layer, h], preferred_element_type=jnp.float32
                )
                keys = projected[:, dim : 2 * dim].astype(jnp.bfloat16)
                values = projected[:, 2 * dim :].astype(jnp.bfloat16)
                qkv[h, here, :dim] = (projected[:, :dim] * dim ** (-0.5)).astype(jnp.bfloat16)
                qkv[h, here, dim : 2 * dim] = keys
                qkv[h, here, 2 * dim :] = values
                prefix[h, block] = running[h].astype(jnp.bfloat16)
                if block + 1 < ctx_size:
                    running[h] = running[h] + lax.dot_general(
                        keys, values, (((0,), (0,)), ((), ())),
                        preferred_element_type=jnp.float32,
                    )
        for d in FAR_FIRST + (0,):
            block = partner(c, d)
            here = rows(block)
            folded = jnp.zeros((tokens, dim), jnp.float32)
            for h in range(heads):
                mine = slice(h * dim, (h + 1) * dim)
                queries = qkv[h, here, :dim]
                values = qkv[h, here, 2 * dim :]
                scores = lax.dot_general(
                    queries, qkv[h, here, dim : 2 * dim], (((1,), (1,)), ((), ())),
                    preferred_element_type=jnp.float32,
                )
                masked = jnp.where(causal, scores, 0.0).astype(jnp.bfloat16)
                mixed = jnp.dot(
                    jnp.concatenate([masked, queries], 1),
                    jnp.concatenate([values, prefix[h, block]], 0),
                    preferred_element_type=jnp.float32,
                )
                spread = lax.rsqrt(row_sums(mixed * mixed) * (1.0 / dim) + epsilon)
                result = (
                    stream[here, mine].astype(jnp.float32)
                    + gains_out[layer, :, mine] * (mixed * spread)
                ).astype(jnp.bfloat16)
                stream[here, mine] = result
                result = result.astype(jnp.float32)
                folded = folded + result * result

            @pl.when(layer < z)
            def _():
                squares[layer + 1, c, pl.ds(block, 1), :] = jnp.sum(folded.T, 0, keepdims=True)

            @pl.when(layer == z)
            def _():
                (out_copy(d) if d else own_out()).start()

        @pl.when(layer < z)
        def _():
            for d in FAR_FIRST:
                sq_copy(layer + 1, d).start()

        for d in FAR_FIRST:
            sq_copy(layer, d).wait_send()
        return carry

    lax.fori_loop(0, z + 1, one_layer, 0)

    own_out().wait()
    for d in FAR_FIRST:
        tok_copy(d).wait_send()
        out_copy(d).wait()
    for stage in plan:
        for sender, layer, to, slot in plan[stage]:
            @pl.when(z == sender)
            def _():
                for copy in w_copies(layer, to, slot, stage == "relay"):
                    copy.wait_send()


def relay(tokens, w_qkv, norm_gain, out_gain):
    ctx_size, sections = lax.axis_size("ctx"), lax.axis_size("pipe")
    rows, features = tokens.shape[1:]
    all_heads, dim = w_qkv.shape[1:3]
    heads = all_heads // ctx_size
    width = heads * dim
    dma = pltpu.SemaphoreType.DMA
    return pl.pallas_call(
        functools.partial(relay_kernel, (ctx_size, sections, heads, dim, rows)),
        out_shape=jax.ShapeDtypeStruct((1,) + tokens.shape, jnp.bfloat16),
        in_specs=[pl.BlockSpec(memory_space=pl.ANY)] * 4,
        out_specs=pl.BlockSpec(memory_space=pl.ANY),
        scratch_shapes=[
            pltpu.VMEM((rows, features), jnp.bfloat16),
            pltpu.VMEM((ctx_size * rows, width), jnp.bfloat16),
            pltpu.VMEM((sections, heads, dim, 3 * dim), jnp.bfloat16),
            pltpu.VMEM((sections, 1, width), jnp.float32),
            pltpu.VMEM((sections, 1, width), jnp.float32),
            pltpu.VMEM((heads, ctx_size * rows, 3 * dim), jnp.bfloat16),
            pltpu.VMEM((heads, ctx_size, dim, dim), jnp.bfloat16),
            pltpu.VMEM((sections, ctx_size, ctx_size, rows), jnp.float32),
            dma((5,)),
            dma((ctx_size,)),
            dma((ctx_size,)),
            dma((sections, ctx_size)),
            dma((sections, ctx_size)),
            dma((sections, 3)),
            dma((sections, 3)),
            dma((ctx_size,)),
            dma((ctx_size,)),
        ],
        compiler_params=pltpu.CompilerParams(collective_id=0, has_side_effects=True),
    )(tokens, w_qkv, norm_gain, out_gain)


def solution(mesh):
    ctx_size, sections = mesh.shape["ctx"], mesh.shape["pipe"]

    def body(tokens, w_qkv, norm_gain, out_gain):
        micro_count, rows = tokens.shape[:2]
        fits = (
            ctx_size == 8
            and sections in (3, 4)
            and micro_count == 1
            and rows == 128
            and w_qkv.shape[1] == 2 * ctx_size
            and w_qkv.shape[2] == 128
        )
        return (relay if fits else shards)(tokens, w_qkv, norm_gain, out_gain)

    placed = (P(None, "ctx", None), P("pipe", None, None, None), P("pipe", None), P("pipe", None))
    return jax.shard_map(
        body, mesh=mesh, in_specs=placed, out_specs=P("pipe", None, "ctx", None), check_vma=False
    )
```

```python
import functools

import jax
import jax.numpy as jnp
from jax import lax
from jax.experimental import pallas as pl
from jax.experimental.pallas import tpu as pltpu
from jax.sharding import PartitionSpec as P

epsilon = 1e-06


def shifted(block, axis, distance):
    devices = range(lax.axis_size(axis))
    route = [(i - distance, i) for i in devices if i - distance in devices]
    return lax.ppermute(block, axis, route)


def run_layer(stream, gain_in, weights, gain_out):
    row_count = stream.shape[0]
    head_count = weights.shape[0]
    head_dim = weights.shape[1]
    widened = stream.astype(jnp.float32)
    normed = (
        widened * lax.rsqrt(jnp.mean(widened * widened, -1, keepdims=True) + epsilon) * gain_in
    ).astype(jnp.bfloat16)
    projected = jnp.einsum(
        "thd,hde->hte",
        normed.reshape(row_count, head_count, head_dim),
        weights,
        preferred_element_type=jnp.float32,
    )
    queries = (projected[..., :head_dim] * head_dim ** (-0.5)).astype(jnp.bfloat16)
    keys_local = projected[..., head_dim : 2 * head_dim].astype(jnp.bfloat16)
    values_local = projected[..., 2 * head_dim :].astype(jnp.bfloat16)
    kv_state = jnp.einsum(
        "hte,htf->hef", keys_local, values_local, preferred_element_type=jnp.float32
    )
    flat_state = kv_state.reshape(1, head_count * head_dim, head_dim)
    spread = lax.all_to_all(
        flat_state.astype(jnp.bfloat16), "ctx", split_axis=1, concat_axis=0, tiled=True
    ).astype(flat_state.dtype)
    running = jnp.cumsum(spread, axis=0)
    lower = jnp.concatenate([jnp.zeros_like(spread[:1]), running[:-1]], axis=0)
    returned = lax.all_to_all(
        lower.astype(jnp.bfloat16), "ctx", split_axis=0, concat_axis=1, tiled=True
    ).astype(lower.dtype)
    prefix = returned.reshape(kv_state.shape)
    scores = jnp.einsum("hte,hse->hts", queries, keys_local, preferred_element_type=jnp.float32)
    positions = jnp.arange(row_count, dtype=jnp.int32)
    causal = positions[:, None] >= positions[None, :]
    masked = jnp.where(causal, scores, 0.0).astype(jnp.bfloat16)
    mixed_heads = jnp.einsum(
        "hts,hsf->htf", masked, values_local, preferred_element_type=jnp.float32
    )
    mixed_heads = mixed_heads + jnp.einsum(
        "hte,hef->htf", queries, prefix.astype(jnp.bfloat16), preferred_element_type=jnp.float32
    )
    mixed_heads = mixed_heads * lax.rsqrt(
        jnp.mean(mixed_heads * mixed_heads, -1, keepdims=True) + epsilon
    )
    branch = jnp.transpose(mixed_heads, (1, 0, 2)).reshape(row_count, head_count * head_dim)
    return (widened + branch * gain_out).astype(jnp.bfloat16)


def shards(tokens, w_qkv, norm_gain, out_gain):
    section_count = lax.axis_size("pipe")
    section_index = lax.axis_index("pipe")
    micro_count = tokens.shape[0]
    hidden_buffer = jnp.zeros(tokens.shape, jnp.bfloat16)
    carried = jnp.zeros(tokens.shape[1:], jnp.bfloat16)
    total_steps = micro_count + section_count - 1
    for tick_index in range(total_steps):
        fresh = tokens[min(tick_index, micro_count - 1)]
        layer_input = jnp.where(section_index == 0, fresh, carried)
        result = run_layer(layer_input, norm_gain[0], w_qkv[0], out_gain[0])
        micro_index = tick_index - section_index
        usable = (micro_index >= 0) & (micro_index < micro_count)
        slot_index = jnp.clip(micro_index, 0, micro_count - 1)
        previous = lax.dynamic_index_in_dim(hidden_buffer, slot_index, 0, keepdims=False)
        hidden_buffer = lax.dynamic_update_index_in_dim(
            hidden_buffer, jnp.where(usable, result, previous), slot_index, 0
        )
        if tick_index + 1 < total_steps:
            carried = shifted(result, "pipe", 1)
    return hidden_buffer[None]


MESH = pl.DeviceIdType.MESH
FAR_FIRST = (6, 7, 2, 4, 3, 5, 1)


def partner(index, flips):
    total = 0
    for bit in (1, 2, 4):
        own = lax.rem(index // bit, 2)
        total = total + (lax.rem(own + 1, 2) if flips & bit else own) * bit
    return total


def lanes_to_rows(row):
    return jnp.broadcast_to(row, (128, row.shape[1])).T


def row_sums(values):
    upper = values.astype(jnp.bfloat16)
    lower = (values - upper.astype(jnp.float32)).astype(jnp.bfloat16)
    ones = jnp.ones((256, 128), jnp.bfloat16)
    return jnp.dot(
        jnp.concatenate([upper, lower], 1), ones, preferred_element_type=jnp.float32
    )


def relay_kernel(
    sizes,
    tok_ref,
    w_ref,
    gin_ref,
    gout_ref,
    out_ref,
    own,
    stream,
    weights,
    gains_in,
    gains_out,
    left,
    right,
    keys,
    values,
    resid,
    row_scale,
    squares,
    local_sem,
    tok_send,
    tok_recv,
    sq_send,
    sq_recv,
    w_send,
    w_recv,
    out_send,
    out_recv,
):
    ctx_size, sections, heads, dim, tokens = sizes
    width = heads * dim
    features = ctx_size * width
    c = lax.axis_index("ctx")
    z = lax.axis_index("pipe")

    def cols(device):
        return pl.ds(pl.multiple_of(device * width, width), width)

    def rows(device):
        return pl.ds(pl.multiple_of(device * tokens, tokens), tokens)

    my_heads = pl.ds(c * heads, heads)

    local = [
        pltpu.make_async_copy(tok_ref.at[0], own, local_sem.at[0]),
        pltpu.make_async_copy(tok_ref.at[0, :, cols(c)], stream.at[rows(c)], local_sem.at[1]),
        pltpu.make_async_copy(w_ref.at[0, my_heads], weights.at[z], local_sem.at[2]),
        pltpu.make_async_copy(gin_ref.at[:, cols(c)], gains_in.at[z], local_sem.at[3]),
        pltpu.make_async_copy(gout_ref.at[:, cols(c)], gains_out.at[z], local_sem.at[4]),
    ]
    for copy in local:
        copy.start()

    barrier = pltpu.get_barrier_semaphore()
    for d in FAR_FIRST:
        pl.semaphore_signal(barrier, 1, device_id=(partner(c, d), z), device_id_type=MESH)
    for step in range(1, sections):
        other = lax.rem(z + step, sections)
        pl.semaphore_signal(barrier, 1, device_id=(c, other), device_id_type=MESH)
    pl.semaphore_wait(barrier, ctx_size + sections - 2)

    def tok_copy(d):
        to = partner(c, d)
        return pltpu.make_async_remote_copy(
            tok_ref.at[0, :, cols(to)], stream.at[rows(c)],
            tok_send.at[d], tok_recv.at[d], device_id=(to, z), device_id_type=MESH,
        )

    def sq_copy(layer, d):
        return pltpu.make_async_remote_copy(
            squares.at[layer, c], squares.at[layer, c],
            sq_send.at[layer, d], sq_recv.at[layer, d],
            device_id=(partner(c, d), z), device_id_type=MESH,
        )

    def w_copies(layer, to, slot, relayed):
        pieces = (
            (weights.at[layer], weights.at[layer]) if relayed else (w_ref.at[0, my_heads], weights.at[layer]),
            (gains_in.at[layer], gains_in.at[layer]) if relayed else (gin_ref.at[:, cols(c)], gains_in.at[layer]),
            (gains_out.at[layer], gains_out.at[layer]) if relayed else (gout_ref.at[:, cols(c)], gains_out.at[layer]),
        )
        return [
            pltpu.make_async_remote_copy(
                source, target, w_send.at[slot, i], w_recv.at[layer, i],
                device_id=(c, to), device_id_type=MESH,
            )
            for i, (source, target) in enumerate(pieces)
        ]

    last = sections - 1
    plan = {"start": [], "early": [], "late": [], "relay": []}
    plan["start"].append((0, 0, last, 0))
    for layer in range(1, last - 1):
        plan["early"].append((layer, layer, last, 0))
    plan["late"].append((last - 1, last - 1, last, 0))
    for layer in range(last - 1):
        for slot, to in enumerate(range(layer + 1, last)):
            if not (layer == 0 and to == last - 1 and last > 2):
                plan["late"].append((layer, layer, to, slot + 1))
    if last > 2:
        plan["relay"].append((last, 0, last - 1, 0))

    def send_weights(stage):
        for sender, layer, to, slot in plan[stage]:
            @pl.when(z == sender)
            def _():
                for copy in w_copies(layer, to, slot, stage == "relay"):
                    copy.start()

    send_weights("start")
    for d in FAR_FIRST:
        tok_copy(d).start()

    local[0].wait()
    folded = jnp.zeros((tokens, 128), jnp.float32)
    for i in range(features // 128):
        piece = own[:, i * 128 : (i + 1) * 128].astype(jnp.float32)
        folded = folded + piece * piece
    total = jnp.sum(folded.T, 0, keepdims=True)
    which = lax.broadcasted_iota(jnp.int32, (ctx_size, tokens), 0)
    squares[0, c] = jnp.where(which == c, jnp.broadcast_to(total, (ctx_size, tokens)), 0.0)
    for d in FAR_FIRST:
        sq_copy(0, d).start()
    for d in FAR_FIRST[:2]:
        tok_copy(d).wait_recv()
    send_weights("early")
    for d in FAR_FIRST[2:]:
        tok_copy(d).wait_recv()
    for copy in local[1:]:
        copy.wait()
    send_weights("late")

    at_row = lax.broadcasted_iota(jnp.int32, (tokens, tokens), 0)
    at_col = lax.broadcasted_iota(jnp.int32, (tokens, tokens), 1)
    causal = at_row >= at_col

    def out_copy(d):
        to = partner(c, d)
        return pltpu.make_async_remote_copy(
            stream.at[rows(to)], out_ref.at[0, 0, :, cols(c)],
            out_send.at[d], out_recv.at[d], device_id=(to, z), device_id_type=MESH,
        )

    def own_out():
        return pltpu.make_async_copy(
            stream.at[rows(c)], out_ref.at[0, 0, :, cols(c)], local_sem.at[0]
        )

    def one_layer(layer, carry):
        @pl.when(layer < z)
        def _():
            for copy in w_copies(layer, z, 0, True):
                copy.wait_recv()

        @pl.when(layer == 0)
        def _():
            send_weights("relay")

        for block in range(ctx_size):
            here = slice(block * tokens, (block + 1) * tokens)
            for h in range(heads):
                mine = slice(h * dim, (h + 1) * dim)
                entering = stream[here, mine]
                resid[here, mine] = entering
                gained = (entering.astype(jnp.float32) * gains_in[layer, :, mine]).astype(
                    jnp.bfloat16
                )
                projected = jnp.dot(
                    gained, weights[layer, h], preferred_element_type=jnp.float32
                )
                queries = projected[:, :dim].astype(jnp.bfloat16)
                turned = projected[:, dim : 2 * dim].astype(jnp.bfloat16).T
                scores = jnp.dot(queries, turned, preferred_element_type=jnp.float32)
                left[h, here, :dim] = jnp.where(causal, scores, 0.0).astype(jnp.bfloat16)
                left[h, here, dim:] = queries
                keys[h, block] = turned
                values[h, here] = projected[:, 2 * dim :]

        for d in FAR_FIRST:
            sq_copy(layer, d).wait_recv()
        scale = lax.rsqrt(jnp.sum(squares[layer], 0) * (1.0 / features) + epsilon)
        running = [jnp.zeros((dim, dim), jnp.float32) for _ in range(heads)]
        for block in range(ctx_size):
            here = slice(block * tokens, (block + 1) * tokens)
            by_row = lanes_to_rows(scale[block : block + 1, :])
            row_scale[here] = by_row * dim ** (-0.5)
            twice = by_row * by_row
            for h in range(heads):
                scaled = (values[h, here] * twice).astype(jnp.bfloat16)
                right[h, block, :tokens] = scaled
                right[h, block, tokens:] = running[h].astype(jnp.bfloat16)
                if block + 1 < ctx_size:
                    running[h] = running[h] + jnp.dot(
                        keys[h, block], scaled, preferred_element_type=jnp.float32
                    )
        for group in (FAR_FIRST[:4], FAR_FIRST[4:] + (0,)):
            for d in group:
                block = partner(c, d)
                here = rows(block)
                folded = jnp.zeros((tokens, dim), jnp.float32)
                for h in range(heads):
                    mine = slice(h * dim, (h + 1) * dim)
                    mixed = row_scale[here] * jnp.dot(
                        left[h, here], right[h, block], preferred_element_type=jnp.float32
                    )
                    spread = lax.rsqrt(row_sums(mixed * mixed) * (1.0 / dim) + epsilon)
                    result = (
                        resid[here, mine].astype(jnp.float32)
                        + gains_out[layer, :, mine] * (mixed * spread)
                    ).astype(jnp.bfloat16)
                    stream[here, mine] = result
                    result = result.astype(jnp.float32)
                    folded = folded + result * result
                squares[layer + 1, c, pl.ds(block, 1), :] = jnp.sum(folded.T, 0, keepdims=True)

            @pl.when(layer == z)
            def _():
                for d in group:
                    (out_copy(d) if d else own_out()).start()

        @pl.when(layer < z)
        def _():
            for d in FAR_FIRST:
                sq_copy(layer + 1, d).start()

        for d in FAR_FIRST:
            sq_copy(layer, d).wait_send()
        return carry

    lax.fori_loop(0, z + 1, one_layer, 0)

    own_out().wait()
    for d in FAR_FIRST:
        tok_copy(d).wait_send()
        out_copy(d).wait()
    for stage in plan:
        for sender, layer, to, slot in plan[stage]:
            @pl.when(z == sender)
            def _():
                for copy in w_copies(layer, to, slot, stage == "relay"):
                    copy.wait_send()


def relay(tokens, w_qkv, norm_gain, out_gain):
    ctx_size, sections = lax.axis_size("ctx"), lax.axis_size("pipe")
    rows, features = tokens.shape[1:]
    all_heads, dim = w_qkv.shape[1:3]
    heads = all_heads // ctx_size
    width = heads * dim
    dma = pltpu.SemaphoreType.DMA
    return pl.pallas_call(
        functools.partial(relay_kernel, (ctx_size, sections, heads, dim, rows)),
        out_shape=jax.ShapeDtypeStruct((1,) + tokens.shape, jnp.bfloat16),
        in_specs=[pl.BlockSpec(memory_space=pl.ANY)] * 4,
        out_specs=pl.BlockSpec(memory_space=pl.ANY),
        scratch_shapes=[
            pltpu.VMEM((rows, features), jnp.bfloat16),
            pltpu.VMEM((ctx_size * rows, width), jnp.bfloat16),
            pltpu.VMEM((sections, heads, dim, 3 * dim), jnp.bfloat16),
            pltpu.VMEM((sections, 1, width), jnp.float32),
            pltpu.VMEM((sections, 1, width), jnp.float32),
            pltpu.VMEM((heads, ctx_size * rows, 2 * dim), jnp.bfloat16),
            pltpu.VMEM((heads, ctx_size, rows + dim, dim), jnp.bfloat16),
            pltpu.VMEM((heads, ctx_size, dim, rows), jnp.bfloat16),
            pltpu.VMEM((heads, ctx_size * rows, dim), jnp.float32),
            pltpu.VMEM((ctx_size * rows, width), jnp.bfloat16),
            pltpu.VMEM((ctx_size * rows, dim), jnp.float32),
            pltpu.VMEM((sections + 1, ctx_size, ctx_size, rows), jnp.float32),
            dma((5,)),
            dma((ctx_size,)),
            dma((ctx_size,)),
            dma((sections, ctx_size)),
            dma((sections, ctx_size)),
            dma((sections, 3)),
            dma((sections, 3)),
            dma((ctx_size,)),
            dma((ctx_size,)),
        ],
        compiler_params=pltpu.CompilerParams(collective_id=0, has_side_effects=True),
    )(tokens, w_qkv, norm_gain, out_gain)


def solution(mesh):
    ctx_size, sections = mesh.shape["ctx"], mesh.shape["pipe"]

    def body(tokens, w_qkv, norm_gain, out_gain):
        micro_count, rows = tokens.shape[:2]
        fits = (
            ctx_size == 8
            and sections in (3, 4)
            and micro_count == 1
            and rows == 128
            and w_qkv.shape[1] == 2 * ctx_size
            and w_qkv.shape[2] == 128
        )
        return (relay if fits else shards)(tokens, w_qkv, norm_gain, out_gain)

    placed = (P(None, "ctx", None), P("pipe", None, None, None), P("pipe", None), P("pipe", None))
    return jax.shard_map(
        body, mesh=mesh, in_specs=placed, out_specs=P("pipe", None, "ctx", None), check_vma=False
    )
```

```python
import functools

import jax
import jax.numpy as jnp
from jax import lax
from jax.experimental import pallas as pl
from jax.experimental.pallas import tpu as pltpu
from jax.sharding import PartitionSpec as P

epsilon = 1e-06


def shifted(block, axis, distance):
    devices = range(lax.axis_size(axis))
    route = [(i - distance, i) for i in devices if i - distance in devices]
    return lax.ppermute(block, axis, route)


def run_layer(stream, gain_in, weights, gain_out):
    row_count = stream.shape[0]
    head_count = weights.shape[0]
    head_dim = weights.shape[1]
    widened = stream.astype(jnp.float32)
    normed = (
        widened * lax.rsqrt(jnp.mean(widened * widened, -1, keepdims=True) + epsilon) * gain_in
    ).astype(jnp.bfloat16)
    projected = jnp.einsum(
        "thd,hde->hte",
        normed.reshape(row_count, head_count, head_dim),
        weights,
        preferred_element_type=jnp.float32,
    )
    queries = (projected[..., :head_dim] * head_dim ** (-0.5)).astype(jnp.bfloat16)
    keys_local = projected[..., head_dim : 2 * head_dim].astype(jnp.bfloat16)
    values_local = projected[..., 2 * head_dim :].astype(jnp.bfloat16)
    kv_state = jnp.einsum(
        "hte,htf->hef", keys_local, values_local, preferred_element_type=jnp.float32
    )
    flat_state = kv_state.reshape(1, head_count * head_dim, head_dim)
    spread = lax.all_to_all(
        flat_state.astype(jnp.bfloat16), "ctx", split_axis=1, concat_axis=0, tiled=True
    ).astype(flat_state.dtype)
    running = jnp.cumsum(spread, axis=0)
    lower = jnp.concatenate([jnp.zeros_like(spread[:1]), running[:-1]], axis=0)
    returned = lax.all_to_all(
        lower.astype(jnp.bfloat16), "ctx", split_axis=0, concat_axis=1, tiled=True
    ).astype(lower.dtype)
    prefix = returned.reshape(kv_state.shape)
    scores = jnp.einsum("hte,hse->hts", queries, keys_local, preferred_element_type=jnp.float32)
    positions = jnp.arange(row_count, dtype=jnp.int32)
    causal = positions[:, None] >= positions[None, :]
    masked = jnp.where(causal, scores, 0.0).astype(jnp.bfloat16)
    mixed_heads = jnp.einsum(
        "hts,hsf->htf", masked, values_local, preferred_element_type=jnp.float32
    )
    mixed_heads = mixed_heads + jnp.einsum(
        "hte,hef->htf", queries, prefix.astype(jnp.bfloat16), preferred_element_type=jnp.float32
    )
    mixed_heads = mixed_heads * lax.rsqrt(
        jnp.mean(mixed_heads * mixed_heads, -1, keepdims=True) + epsilon
    )
    branch = jnp.transpose(mixed_heads, (1, 0, 2)).reshape(row_count, head_count * head_dim)
    return (widened + branch * gain_out).astype(jnp.bfloat16)


def shards(tokens, w_qkv, norm_gain, out_gain):
    section_count = lax.axis_size("pipe")
    section_index = lax.axis_index("pipe")
    micro_count = tokens.shape[0]
    hidden_buffer = jnp.zeros(tokens.shape, jnp.bfloat16)
    carried = jnp.zeros(tokens.shape[1:], jnp.bfloat16)
    total_steps = micro_count + section_count - 1
    for tick_index in range(total_steps):
        fresh = tokens[min(tick_index, micro_count - 1)]
        layer_input = jnp.where(section_index == 0, fresh, carried)
        result = run_layer(layer_input, norm_gain[0], w_qkv[0], out_gain[0])
        micro_index = tick_index - section_index
        usable = (micro_index >= 0) & (micro_index < micro_count)
        slot_index = jnp.clip(micro_index, 0, micro_count - 1)
        previous = lax.dynamic_index_in_dim(hidden_buffer, slot_index, 0, keepdims=False)
        hidden_buffer = lax.dynamic_update_index_in_dim(
            hidden_buffer, jnp.where(usable, result, previous), slot_index, 0
        )
        if tick_index + 1 < total_steps:
            carried = shifted(result, "pipe", 1)
    return hidden_buffer[None]


MESH = pl.DeviceIdType.MESH
FAR_FIRST = (6, 7, 2, 4, 3, 5, 1)


def partner(index, flips):
    total = 0
    for bit in (1, 2, 4):
        own = lax.rem(index // bit, 2)
        total = total + (lax.rem(own + 1, 2) if flips & bit else own) * bit
    return total


def lanes_to_rows(row):
    return jnp.broadcast_to(row, (128, row.shape[1])).T


def row_sums(values):
    upper = values.astype(jnp.bfloat16)
    lower = (values - upper.astype(jnp.float32)).astype(jnp.bfloat16)
    ones = jnp.ones((256, 128), jnp.bfloat16)
    return jnp.dot(
        jnp.concatenate([upper, lower], 1), ones, preferred_element_type=jnp.float32
    )


def relay_kernel(
    sizes,
    tok_ref,
    w_ref,
    gin_ref,
    gout_ref,
    out_ref,
    own,
    stream,
    weights,
    gains_in,
    gains_out,
    left,
    right,
    keys,
    values,
    resid,
    row_scale,
    squares,
    local_sem,
    tok_send,
    tok_recv,
    sq_send,
    sq_recv,
    w_send,
    w_recv,
    out_send,
    out_recv,
):
    ctx_size, sections, heads, dim, tokens = sizes
    width = heads * dim
    features = ctx_size * width
    c = lax.axis_index("ctx")
    z = lax.axis_index("pipe")

    def cols(device):
        return pl.ds(pl.multiple_of(device * width, width), width)

    def rows(device):
        return pl.ds(pl.multiple_of(device * tokens, tokens), tokens)

    my_heads = pl.ds(c * heads, heads)

    local = [
        pltpu.make_async_copy(tok_ref.at[0], own, local_sem.at[0]),
        pltpu.make_async_copy(tok_ref.at[0, :, cols(c)], stream.at[rows(c)], local_sem.at[1]),
        pltpu.make_async_copy(w_ref.at[0, my_heads], weights.at[z], local_sem.at[2]),
        pltpu.make_async_copy(gin_ref.at[:, cols(c)], gains_in.at[z], local_sem.at[3]),
        pltpu.make_async_copy(gout_ref.at[:, cols(c)], gains_out.at[z], local_sem.at[4]),
    ]
    for copy in local:
        copy.start()

    barrier = pltpu.get_barrier_semaphore()
    for d in FAR_FIRST:
        pl.semaphore_signal(barrier, 1, device_id=(partner(c, d), z), device_id_type=MESH)
    for step in range(1, sections):
        other = lax.rem(z + step, sections)
        pl.semaphore_signal(barrier, 1, device_id=(c, other), device_id_type=MESH)
    pl.semaphore_wait(barrier, ctx_size + sections - 2)

    def tok_copy(d):
        to = partner(c, d)
        return pltpu.make_async_remote_copy(
            tok_ref.at[0, :, cols(to)], stream.at[rows(c)],
            tok_send.at[d], tok_recv.at[d], device_id=(to, z), device_id_type=MESH,
        )

    def sq_copy(layer, d):
        return pltpu.make_async_remote_copy(
            squares.at[layer, c], squares.at[layer, c],
            sq_send.at[layer, d], sq_recv.at[layer, d],
            device_id=(partner(c, d), z), device_id_type=MESH,
        )

    def w_copies(layer, to, slot, relayed):
        pieces = [
            (weights.at[layer, h] if relayed else w_ref.at[0, c * heads + h], weights.at[layer, h])
            for h in range(heads)
        ]
        for gain_ref, gain in ((gin_ref, gains_in), (gout_ref, gains_out)):
            pieces.append((gain.at[layer] if relayed else gain_ref.at[:, cols(c)], gain.at[layer]))
        return [
            pltpu.make_async_remote_copy(
                source, target, w_send.at[slot, i], w_recv.at[layer, i],
                device_id=(c, to), device_id_type=MESH,
            )
            for i, (source, target) in enumerate(pieces)
        ]

    last = sections - 1
    plan = {"start": [], "early": [], "late": [], "relay": []}
    plan["start"].append((0, 0, last, 0))
    for layer in range(1, last - 1):
        plan["early"].append((layer, layer, last, 0))
    plan["late"].append((last - 1, last - 1, last, 0))
    for layer in range(last - 1):
        for slot, to in enumerate(range(layer + 1, last)):
            if not (layer == 0 and to == last - 1 and last > 2):
                plan["late"].append((layer, layer, to, slot + 1))
    if last > 2:
        plan["relay"].append((last, 0, last - 1, 0))

    def send_weights(stage):
        for sender, layer, to, slot in plan[stage]:
            @pl.when(z == sender)
            def _():
                for copy in w_copies(layer, to, slot, stage == "relay"):
                    copy.start()

    send_weights("start")
    for d in FAR_FIRST:
        tok_copy(d).start()

    local[0].wait()
    folded = jnp.zeros((tokens, 128), jnp.float32)
    for i in range(features // 128):
        piece = own[:, i * 128 : (i + 1) * 128].astype(jnp.float32)
        folded = folded + piece * piece
    total = jnp.sum(folded.T, 0, keepdims=True)
    which = lax.broadcasted_iota(jnp.int32, (ctx_size, tokens), 0)
    squares[0, c] = jnp.where(which == c, jnp.broadcast_to(total, (ctx_size, tokens)), 0.0)
    for d in FAR_FIRST:
        sq_copy(0, d).start()
    for d in (1, 6):
        tok_copy(d).wait_recv()
    send_weights("early")
    tok_copy(7).wait_recv()
    for copy in local[1:]:
        copy.wait()
    send_weights("late")

    def await_weights(layer):
        for copy in w_copies(layer, z, 0, True):
            copy.wait_recv()

    @pl.when(jnp.logical_and(z > 0, z < last))
    def _():
        await_weights(0)

    @pl.when(z == last)
    def _():
        if last > 2:
            onward = w_copies(0, last - 1, 0, True)
            for arriving, leaving in zip(w_copies(0, z, 0, True), onward):
                arriving.wait_recv()
                leaving.start()
        else:
            await_weights(0)

    at_row = lax.broadcasted_iota(jnp.int32, (tokens, tokens), 0)
    at_col = lax.broadcasted_iota(jnp.int32, (tokens, tokens), 1)
    causal = at_row >= at_col

    def out_copy(d):
        to = partner(c, d)
        return pltpu.make_async_remote_copy(
            stream.at[rows(to)], out_ref.at[0, 0, :, cols(c)],
            out_send.at[d], out_recv.at[d], device_id=(to, z), device_id_type=MESH,
        )

    def own_out():
        return pltpu.make_async_copy(
            stream.at[rows(c)], out_ref.at[0, 0, :, cols(c)], local_sem.at[0]
        )

    def project(layer, block):
        here = rows(block)
        for h in range(heads):
            mine = slice(h * dim, (h + 1) * dim)
            entering = stream[here, mine]
            resid[here, mine] = entering
            gained = (entering.astype(jnp.float32) * gains_in[layer, :, mine]).astype(
                jnp.bfloat16
            )
            projected = jnp.dot(gained, weights[layer, h], preferred_element_type=jnp.float32)
            queries = projected[:, :dim].astype(jnp.bfloat16)
            turned = projected[:, dim : 2 * dim].astype(jnp.bfloat16).T
            scores = jnp.dot(queries, turned, preferred_element_type=jnp.float32)
            left[h, here, :dim] = jnp.where(causal, scores, 0.0).astype(jnp.bfloat16)
            left[h, here, dim:] = queries
            keys[h, block] = turned
            values[h, here] = projected[:, 2 * dim :]

    for pair in ((0, 1), (6, 7), (2, 4), (3, 5)):
        for d in pair:
            if d in (2, 3, 4, 5):
                tok_copy(d).wait_recv()
        for d in pair:
            project(0, partner(c, d))

    def one_layer(layer, carry):
        for d in FAR_FIRST:
            sq_copy(layer, d).wait_recv()
        scale = lax.rsqrt(jnp.sum(squares[layer], 0) * (1.0 / features) + epsilon)
        running = [jnp.zeros((dim, dim), jnp.float32) for _ in range(heads)]
        for block in range(ctx_size):
            here = slice(block * tokens, (block + 1) * tokens)
            by_row = lanes_to_rows(scale[block : block + 1, :])
            row_scale[here] = by_row * dim ** (-0.5)
            twice = by_row * by_row
            for h in range(heads):
                scaled = (values[h, here] * twice).astype(jnp.bfloat16)
                right[h, block, :tokens] = scaled
                right[h, block, tokens:] = running[h].astype(jnp.bfloat16)
                if block + 1 < ctx_size:
                    running[h] = running[h] + jnp.dot(
                        keys[h, block], scaled, preferred_element_type=jnp.float32
                    )
        for group in (FAR_FIRST[:4], FAR_FIRST[4:] + (0,)):
            for d in group:
                block = partner(c, d)
                here = rows(block)
                folded = jnp.zeros((tokens, dim), jnp.float32)
                for h in range(heads):
                    mine = slice(h * dim, (h + 1) * dim)
                    mixed = row_scale[here] * jnp.dot(
                        left[h, here], right[h, block], preferred_element_type=jnp.float32
                    )
                    spread = lax.rsqrt(row_sums(mixed * mixed) * (1.0 / dim) + epsilon)
                    result = (
                        resid[here, mine].astype(jnp.float32)
                        + gains_out[layer, :, mine] * (mixed * spread)
                    ).astype(jnp.bfloat16)
                    stream[here, mine] = result
                    result = result.astype(jnp.float32)
                    folded = folded + result * result
                squares[layer + 1, c, pl.ds(block, 1), :] = jnp.sum(folded.T, 0, keepdims=True)

            @pl.when(layer == z)
            def _():
                for d in group:
                    (out_copy(d) if d else own_out()).start()

        @pl.when(layer < z)
        def _():
            for d in FAR_FIRST:
                sq_copy(layer + 1, d).start()

            @pl.when(layer + 1 < z)
            def _():
                await_weights(layer + 1)

            for block in range(ctx_size):
                project(layer + 1, block)

        for d in FAR_FIRST:
            sq_copy(layer, d).wait_send()
        return carry

    lax.fori_loop(0, z + 1, one_layer, 0)

    own_out().wait()
    for d in FAR_FIRST:
        tok_copy(d).wait_send()
        out_copy(d).wait()
    for stage in plan:
        for sender, layer, to, slot in plan[stage]:
            @pl.when(z == sender)
            def _():
                for copy in w_copies(layer, to, slot, stage == "relay"):
                    copy.wait_send()


def relay(tokens, w_qkv, norm_gain, out_gain):
    ctx_size, sections = lax.axis_size("ctx"), lax.axis_size("pipe")
    rows, features = tokens.shape[1:]
    all_heads, dim = w_qkv.shape[1:3]
    heads = all_heads // ctx_size
    width = heads * dim
    dma = pltpu.SemaphoreType.DMA
    return pl.pallas_call(
        functools.partial(relay_kernel, (ctx_size, sections, heads, dim, rows)),
        out_shape=jax.ShapeDtypeStruct((1,) + tokens.shape, jnp.bfloat16),
        in_specs=[pl.BlockSpec(memory_space=pl.ANY)] * 4,
        out_specs=pl.BlockSpec(memory_space=pl.ANY),
        scratch_shapes=[
            pltpu.VMEM((rows, features), jnp.bfloat16),
            pltpu.VMEM((ctx_size * rows, width), jnp.bfloat16),
            pltpu.VMEM((sections, heads, dim, 3 * dim), jnp.bfloat16),
            pltpu.VMEM((sections, 1, width), jnp.float32),
            pltpu.VMEM((sections, 1, width), jnp.float32),
            pltpu.VMEM((heads, ctx_size * rows, 2 * dim), jnp.bfloat16),
            pltpu.VMEM((heads, ctx_size, rows + dim, dim), jnp.bfloat16),
            pltpu.VMEM((heads, ctx_size, dim, rows), jnp.bfloat16),
            pltpu.VMEM((heads, ctx_size * rows, dim), jnp.float32),
            pltpu.VMEM((ctx_size * rows, width), jnp.bfloat16),
            pltpu.VMEM((ctx_size * rows, dim), jnp.float32),
            pltpu.VMEM((sections + 1, ctx_size, ctx_size, rows), jnp.float32),
            dma((5,)),
            dma((ctx_size,)),
            dma((ctx_size,)),
            dma((sections, ctx_size)),
            dma((sections, ctx_size)),
            dma((sections, heads + 2)),
            dma((sections, heads + 2)),
            dma((ctx_size,)),
            dma((ctx_size,)),
        ],
        compiler_params=pltpu.CompilerParams(collective_id=0, has_side_effects=True),
    )(tokens, w_qkv, norm_gain, out_gain)


def solution(mesh):
    ctx_size, sections = mesh.shape["ctx"], mesh.shape["pipe"]

    def body(tokens, w_qkv, norm_gain, out_gain):
        micro_count, rows = tokens.shape[:2]
        fits = (
            ctx_size == 8
            and sections in (3, 4)
            and micro_count == 1
            and rows == 128
            and w_qkv.shape[1] == 2 * ctx_size
            and w_qkv.shape[2] == 128
        )
        return (relay if fits else shards)(tokens, w_qkv, norm_gain, out_gain)

    placed = (P(None, "ctx", None), P("pipe", None, None, None), P("pipe", None), P("pipe", None))
    return jax.shard_map(
        body, mesh=mesh, in_specs=placed, out_specs=P("pipe", None, "ctx", None), check_vma=False
    )
```
